256 devices in a mesh: xy: 32 (over z, x_lo, core), gz: 8 (over y, x_hi).
Axes of the slice: x: 4 (x_hi: 2, x_lo: 2; x = x_hi * 2 + x_lo), y: 4, z: 8, core: 2. Of those that a mesh axis runs over, the one named last changes fastest.
Arguments:
- file_data: float32 [512, 64, 8192], P('gz', None, 'xy')
- factor: float32 [512, 256], P('gz'), may hold values from -0.25 to 0.25
- block_owner: int32 [64], replicated, may hold values from 0 to 31, as said below
- block_offset: int32 [64], replicated, may hold values from 0 to 128, as said below
Outputs:
- gram: float32 [512, 512], P('gz')
- core: float32 [256, 64, 8192], P('gz', None, 'xy')
The draws below stay inside these ranges and needn't reach their ends.
Inputs may be any that keep to these rules, and one draw needn't show every extreme that they name: `block_owner`: block b of device d (b = d * 2 + j) is owned by d - 1, d or d + 1 modulo 32. Every index of xy owns exactly 2 blocks. `block_offset`: offsets are multiples of 128; the blocks of one owner take distinct offsets, so every file slot is named once.
All inputs are finite; a program needn't handle non-finite values.
Results may differ from the reference program's by a relative error of at most 0.00007.
Values sent between devices are 32-bit elements; how exact they have to be, the bound alone decides.
A program may use at most 128 MiB of HBM per device.

```python
import jax
import jax.numpy as jnp
from jax import lax

Z = 512
SPECIES = 64
RANK = 256
BLOCKS_DEV = 2
FILE_BLOCKS = 2
FILE_ROWS = 8192
N_XY = 32


def block_tables(key):
    key = jax.random.fold_in(key, 11)
    parity_key, keep_key, perm_key = jax.random.split(key, 3)
    half = N_XY // 2
    middle = N_XY // 2
    parity = jax.random.randint(parity_key, (BLOCKS_DEV,), 0, 2)
    parity = parity.at[0].set(1).at[1].set(0)
    keep = jax.random.randint(keep_key, (BLOCKS_DEV, half), 0, 2)
    column = jnp.arange(BLOCKS_DEV)[:, None]
    pair_index = jnp.arange(half)[None, :]
    first_forced = (pair_index == half - 1) | (pair_index == (middle - 2) // 2)
    second_forced = (pair_index == 0) | (pair_index == middle // 2) | (pair_index == half - 1)
    keep = jnp.where((column == 0) & first_forced, 1, keep)
    keep = jnp.where((column == 1) & second_forced, 1, keep)
    device = jnp.arange(N_XY)[:, None]
    moved = (device - parity[None, :]) % N_XY
    pair = moved // 2
    position = moved % 2
    kept = keep[jnp.arange(BLOCKS_DEV)[None, :], pair]
    sides = jnp.where(position == 0, 1, -1) * kept
    owner = ((device + sides) % N_XY).reshape(-1)
    count = owner.shape[0]
    earlier = jnp.arange(count)[None, :] < jnp.arange(count)[:, None]
    same = owner[None, :] == owner[:, None]
    ranks = jnp.sum((earlier & same).astype(jnp.int32), axis=1)
    perms = jax.vmap(lambda k: jax.random.permutation(k, FILE_BLOCKS))(jax.random.split(perm_key, N_XY))
    offset = perms[owner, ranks] * 128
    return (owner.astype(jnp.int32), offset.astype(jnp.int32))


def draw_block_owner(key, part):
    return block_tables(key)[0]


def draw_block_offset(key, part):
    return block_tables(key)[1]


def draw_file_data(key, part):
    keys = jax.random.split(key, 3)
    zscale = jnp.exp(jax.random.uniform(keys[0], (Z, 1, 1), jnp.float32, -0.7, 0.7))
    sscale = jnp.exp(jax.random.uniform(keys[1], (1, SPECIES, 1), jnp.float32, -0.7, 0.7))
    values = jax.random.normal(keys[2], (Z, SPECIES, FILE_ROWS), jnp.float32)
    return (values * zscale * sscale).astype(jnp.float32)


def steps_of(key, extent, cuts, smallest, top_value):
    gain = 1.0
    for axis_at, parts in cuts:
        heights = jax.random.uniform(jax.random.fold_in(jax.random.fold_in(key, 6), axis_at), (parts,), jnp.float32, smallest / len(cuts), top_value / len(cuts))
        gain = gain * jnp.repeat(jnp.exp(heights), extent[axis_at] // parts).reshape((-1,) + (1,) * (len(extent) - 1 - axis_at))
    return gain


def centred(key, dims, scale, most, cuts=(), kind=jnp.bfloat16):
    gain = steps_of(key, dims, cuts, -0.22, 0.18) if cuts else 1.0
    array = jax.random.normal(key, dims, jnp.float32) * scale * gain
    return jnp.minimum(jnp.maximum(array, -most), most).astype(kind)


def setup_inputs(seed: int = 0) -> dict:
    seeds = jax.random.split(jax.random.key(seed), 5)
    file_data = draw_file_data(jax.random.fold_in(seeds[4], 71), 0)
    factor = centred(seeds[1], (Z, RANK), Z ** -0.5, 0.25, ((0, 8),), jnp.float32)
    block_owner = draw_block_owner(jax.random.fold_in(seeds[4], 71), 0)
    block_offset = draw_block_offset(jax.random.fold_in(seeds[4], 71), 0)
    return {"file_data": file_data, "factor": factor, "block_owner": block_owner, "block_offset": block_offset}


def reference(file_data, factor, block_owner, block_offset):
    file_dev = file_data.shape[2] // N_XY
    starts = block_owner.astype(jnp.int32) * file_dev + block_offset.astype(jnp.int32)
    index = (starts[:, None] + jnp.arange(128, dtype=jnp.int32)[None, :]).reshape(-1)
    field = jnp.take(file_data, index, axis=2)
    scale = 1.0 / (index.shape[0] * file_data.shape[1])
    gram = jnp.einsum("zcs,wcs->zw", field, field, precision=lax.Precision.HIGHEST) * scale
    core = jnp.einsum("zr,zcs->rcs", factor, field, precision=lax.Precision.HIGHEST)
    return gram, core
```

```python
import jax
import jax.numpy as jnp
from jax import lax
from jax.sharding import PartitionSpec as P

BLOCKS_DEV = 2


def shifted(array, axis, by):
    length = lax.axis_size(axis)
    return lax.ppermute(array, axis, [(i, (i + by) % length) for i in range(length)])


def take_block(buffer, offset):
    return lax.dynamic_slice_in_dim(buffer, offset, 128, 2)


def rebalance(buffer, block_owner, block_offset):
    devices = lax.axis_size("xy")
    myself = lax.axis_index("xy")
    lower_peer = (myself + devices - 1) % devices
    upper_peer = (myself + 1) % devices

    def outgoing(target):
        pieces = []
        for j in range(BLOCKS_DEV):
            pieces.append(take_block(buffer, block_offset[target * BLOCKS_DEV + j]))
        return jnp.concatenate(pieces, axis=2)

    from_lower = shifted(outgoing(upper_peer), "xy", 1)
    from_upper = shifted(outgoing(lower_peer), "xy", -1)
    blocks = []
    for j in range(BLOCKS_DEV):
        owner = block_owner[myself * BLOCKS_DEV + j]
        offset = block_offset[myself * BLOCKS_DEV + j]
        local_block = take_block(buffer, offset)
        lower_block = from_lower[:, :, j * 128 : (j + 1) * 128]
        upper_block = from_upper[:, :, j * 128 : (j + 1) * 128]
        remote = jnp.where(owner == lower_peer, lower_block, upper_block)
        blocks.append(jnp.where(owner == myself, local_block, remote))
    return jnp.concatenate(blocks, axis=2)


def halves(x):
    high = lax.reduce_precision(x, exponent_bits=8, mantissa_bits=7)
    low = x - high
    return high.astype(jnp.bfloat16), low.astype(jnp.bfloat16)


def dot(spec, a, b):
    return jnp.einsum(spec, a, b, preferred_element_type=jnp.float32)


def local(file_data, factor, block_owner, block_offset):
    whole_factor = lax.all_gather(factor, "gz", axis=0, tiled=True)
    swapped = lax.all_to_all(file_data, "gz", split_axis=1, concat_axis=0, tiled=True)
    scale = 1.0 / (BLOCKS_DEV * 128 * lax.axis_size("xy") * file_data.shape[1])
    high, low = halves(swapped)
    factor_high, factor_low = halves(whole_factor)
    core_part = (
        dot("zr,zcs->rcs", factor_high, high)
        + dot("zr,zcs->rcs", factor_high, low)
        + dot("zr,zcs->rcs", factor_low, high)
    )
    core = lax.all_to_all(core_part, "gz", split_axis=0, concat_axis=1, tiled=True)
    cross = dot("zcs,wcs->zw", high, low)
    partial_gram = (dot("zcs,wcs->zw", high, high) + (cross + cross.T)) * scale
    gram = lax.psum_scatter(partial_gram, "gz", scatter_dimension=0, tiled=True)
    gram = lax.psum(gram, "xy")
    core = rebalance(core, block_owner, block_offset)
    return (gram, core)


def solution(mesh):
    return jax.shard_map(
        local,
        mesh=mesh,
        in_specs=(P("gz", None, "xy"), P("gz", None), P(), P()),
        out_specs=(P("gz", None), P("gz", None, "xy")),
        check_vma=False,
    )
```

```python
import functools

import jax
import jax.numpy as jnp
from jax import lax
from jax.experimental import pallas as pl
from jax.experimental.pallas import tpu as pltpu
from jax.sharding import PartitionSpec as P

MESH = pl.DeviceIdType.MESH
GZ = 8
LANES = 128
SWAP_ORDER = (4, 1, 6, 2, 7, 5, 3)
SCATTER_ORDER = (
    (6, 1), (0, 0), (5, 0), (3, 0), (2, 0), (4, 1), (4, 0), (1, 0),
    (5, 1), (2, 1), (3, 1), (7, 1), (1, 1), (7, 0), (6, 0),
)


def mirrored(offset):
    return (4 - offset // 2) % 4 * 2 + offset % 2


def place():
    d = lax.axis_index("xy")
    g = lax.axis_index("gz")
    return d, g, lax.rem(d, 2)


def by_core(core, offset):
    other = mirrored(offset)
    return offset if offset == other else offset * (1 - core) + other * core


def peer(g, offset):
    if isinstance(offset, int):
        dy, dx = offset // 2, offset % 2
    else:
        dy, dx = lax.div(offset, 2), lax.rem(offset, 2)
    return lax.rem(lax.div(g, 2) + dy, 4) * 2 + lax.rem(lax.rem(g, 2) + dx, 2)


def greet(peers):
    barrier = pltpu.get_barrier_semaphore()
    for where in peers:
        pl.semaphore_signal(barrier, inc=1, device_id=where, device_id_type=MESH)
    pl.semaphore_wait(barrier, len(peers))


def swap_kernel(x_ref, f_ref, out_ref, factor_ref, local_sem, x_send, x_recv, f_send, f_recv):
    d, g, core = place()
    greet([{"xy": d, "gz": peer(g, o)} for o in range(1, GZ)])
    copies = []
    for step in SWAP_ORDER:
        o = by_core(core, step)
        to = peer(g, o)
        copies.append(
            pltpu.make_async_remote_copy(
                src_ref=x_ref.at[:, pl.ds(pl.multiple_of(to * 8, 8), 8), :],
                dst_ref=out_ref.at[g],
                send_sem=x_send.at[o],
                recv_sem=x_recv.at[o],
                device_id={"xy": d, "gz": to},
                device_id_type=MESH,
            )
        )
        copies.append(
            pltpu.make_async_remote_copy(
                src_ref=f_ref,
                dst_ref=factor_ref.at[g],
                send_sem=f_send.at[o],
                recv_sem=f_recv.at[o],
                device_id={"xy": d, "gz": to},
                device_id_type=MESH,
            )
        )
    for copy in copies:
        copy.start()
    mine = x_ref.at[:, pl.ds(pl.multiple_of(g * 8, 8), 8), :]
    own = pltpu.make_async_copy(mine, out_ref.at[g], local_sem.at[0])
    own_factor = pltpu.make_async_copy(f_ref, factor_ref.at[g], local_sem.at[1])
    own.start()
    own_factor.start()
    own.wait()
    own_factor.wait()
    for copy in copies:
        copy.wait()


def swap(field, factor):
    planes, species, points = field.shape
    return pl.pallas_call(
        swap_kernel,
        out_shape=(
            jax.ShapeDtypeStruct((GZ, planes, species // GZ, points), jnp.float32),
            jax.ShapeDtypeStruct((GZ, *factor.shape), jnp.float32),
        ),
        in_specs=[pl.BlockSpec(memory_space=pl.ANY)] * 2,
        out_specs=[pl.BlockSpec(memory_space=pltpu.VMEM)] * 2,
        scratch_shapes=[
            pltpu.SemaphoreType.DMA((2,)),
            pltpu.SemaphoreType.DMA((GZ,)),
            pltpu.SemaphoreType.DMA((GZ,)),
            pltpu.SemaphoreType.DMA((GZ,)),
            pltpu.SemaphoreType.DMA((GZ,)),
        ],
        compiler_params=pltpu.CompilerParams(collective_id=0, has_side_effects=True),
        name="swap",
    )(field, factor)


def halves(x):
    high = x.astype(jnp.bfloat16)
    return high, (x - high.astype(jnp.float32)).astype(jnp.bfloat16)


def product_kernel(scale, x_ref, f_ref, gram_ref, core_ref, high_ref, low_ref):
    z = x_ref.shape[0] * x_ref.shape[1]
    species, points = x_ref.shape[2:]
    f_high, f_low = halves(f_ref[...])
    dot = functools.partial(jnp.dot, preferred_element_type=jnp.float32)
    for c in range(species):
        x = x_ref[:, :, c, :].reshape(z, points)
        high, low = halves(x)
        high_ref[:, c * points : (c + 1) * points] = high
        low_ref[:, c * points : (c + 1) * points] = low
        core_ref[c] = dot(f_high, high) + dot(f_high, low) + dot(f_low, high)
    across = (((1,), (1,)), ((), ()))
    high = high_ref[...]
    gram = lax.dot_general(high, high, across, preferred_element_type=jnp.float32)
    cross = lax.dot_general(high, low_ref[...], across, preferred_element_type=jnp.float32)
    gram_ref[...] = (gram + (cross + cross.T)) * scale


def products(swapped, factor_t, scale):
    groups, planes, species, points = swapped.shape
    z, rank = groups * planes, factor_t.shape[0]
    return pl.pallas_call(
        functools.partial(product_kernel, scale),
        out_shape=(
            jax.ShapeDtypeStruct((z, z), jnp.float32),
            jax.ShapeDtypeStruct((species, rank, points), jnp.float32),
        ),
        in_specs=[pl.BlockSpec(memory_space=pltpu.VMEM)] * 2,
        out_specs=[pl.BlockSpec(memory_space=pltpu.VMEM)] * 2,
        scratch_shapes=[
            pltpu.VMEM((z, species * points), jnp.bfloat16),
            pltpu.VMEM((z, species * points), jnp.bfloat16),
        ],
        name="products",
    )(swapped, factor_t)


def scatter_kernel(core_ref, out_ref, local_sem, send, recv, pair_send, pair_recv):
    d, g, core = place()
    beyond = lax.rem(d + 31 + 2 * core, 32)
    pair = d + 1 - 2 * core
    rows = core_ref.shape[1] // GZ

    def part(to):
        return core_ref.at[:, pl.ds(pl.multiple_of(to * rows, rows), rows), :]

    greet(
        [{"xy": d, "gz": peer(g, o)} for o in range(1, GZ)]
        + [{"xy": beyond, "gz": peer(g, o)} for o in range(GZ)]
        + [{"xy": pair, "gz": g}]
    )
    copies = {}
    for step, kind in SCATTER_ORDER:
        o = by_core(core, step)
        to = peer(g, o)
        copies[step, kind] = pltpu.make_async_remote_copy(
            src_ref=part(to),
            dst_ref=out_ref.at[kind, g],
            send_sem=send.at[2 * o + kind],
            recv_sem=recv.at[2 * o + kind],
            device_id={"xy": d if kind else beyond, "gz": to},
            device_id_type=MESH,
        )
        copies[step, kind].start()

    def to_pair(source, slot, src_ref):
        return pltpu.make_async_remote_copy(
            src_ref=src_ref,
            dst_ref=out_ref.at[2, source],
            send_sem=pair_send.at[slot],
            recv_sem=pair_recv.at[slot],
            device_id={"xy": pair, "gz": g},
            device_id_type=MESH,
        )

    passed = [to_pair(g, 0, part(g))]
    passed[0].start()
    own = pltpu.make_async_copy(part(g), out_ref.at[1, g], local_sem)
    own.start()
    for step, kind in SCATTER_ORDER:
        copies[step, kind].wait_recv()
        if kind == 1:
            source = peer(g, by_core(core, mirrored(step)))
            passed.append(to_pair(source, step, out_ref.at[1, source]))
            passed[-1].start()
    own.wait()
    for copy in copies.values():
        copy.wait_send()
    for copy in passed:
        copy.wait()


def scatter(core):
    species, rank, points = core.shape
    return pl.pallas_call(
        scatter_kernel,
        out_shape=jax.ShapeDtypeStruct((3, GZ, species, rank // GZ, points), jnp.float32),
        in_specs=[pl.BlockSpec(memory_space=pltpu.VMEM)],
        out_specs=pl.BlockSpec(memory_space=pl.ANY),
        scratch_shapes=[
            pltpu.SemaphoreType.DMA,
            pltpu.SemaphoreType.DMA((2 * GZ,)),
            pltpu.SemaphoreType.DMA((2 * GZ,)),
            pltpu.SemaphoreType.DMA((GZ,)),
            pltpu.SemaphoreType.DMA((GZ,)),
        ],
        compiler_params=pltpu.CompilerParams(collective_id=1, has_side_effects=True),
        cost_estimate=pl.CostEstimate(flops=0, transcendentals=0, bytes_accessed=200_000_000),
        name="scatter",
    )(core)


def place_kernel(which_ref, half_ref, in_ref, out_ref):
    for c in range(in_ref.shape[2]):
        out_ref[:, c, :] = in_ref[0, 0, c]


def placed(candidates, which, half):
    _, groups, species, rows, points = candidates.shape
    grid_spec = pltpu.PrefetchScalarGridSpec(
        num_scalar_prefetch=2,
        grid=(groups, points // LANES),
        in_specs=[
            pl.BlockSpec(
                (1, 1, species, rows, LANES),
                lambda i, j, which, half: (which[j], i, 0, 0, half[j]),
            )
        ],
        out_specs=pl.BlockSpec((rows, species, LANES), lambda i, j, which, half: (0, i, j)),
    )
    return pl.pallas_call(
        place_kernel,
        out_shape=jax.ShapeDtypeStruct((rows, groups * species, points), jnp.float32),
        grid_spec=grid_spec,
        name="placed",
    )(which, half, candidates)


def local(file_data, factor, block_owner, block_offset):
    myself = lax.axis_index("xy")
    blocks = file_data.shape[2] // LANES
    owner = lax.dynamic_slice_in_dim(block_owner, myself * blocks, blocks)
    half = lax.dynamic_slice_in_dim(block_offset, myself * blocks, blocks) // LANES
    pair = myself + 1 - 2 * (myself % 2)
    which = jnp.where(owner == myself, 1, jnp.where(owner == pair, 2, 0)).astype(jnp.int32)

    swapped, factors = swap(file_data, factor)
    factor_t = factors.reshape(-1, factor.shape[1]).T
    scale = 1.0 / (file_data.shape[2] * lax.axis_size("xy") * file_data.shape[1])
    partial_gram, core_part = products(swapped, factor_t, scale)
    planes = file_data.shape[0]
    tiles = lax.all_to_all(
        partial_gram.reshape(GZ, planes, partial_gram.shape[1]), "gz", 0, 0, tiled=True
    )
    gram = lax.all_gather(jnp.sum(tiles, axis=0), "xy").sum(axis=0)
    core_part, tiles = lax.optimization_barrier((core_part, tiles))
    core = placed(scatter(core_part), which, half)
    return (gram, core)


def solution(mesh):
    return jax.shard_map(
        local,
        mesh=mesh,
        in_specs=(P("gz", None, "xy"), P("gz", None), P(), P()),
        out_specs=(P("gz", None), P("gz", None, "xy")),
        check_vma=False,
    )
```
